256 devices in a mesh: cells: 64 (over y, z_lo, x), bands: 4 (over z_hi, core).
Axes of the slice: x: 4, y: 4, z: 8 (z_hi: 2, z_lo: 4; z = z_hi * 4 + z_lo), core: 2. Of those that a mesh axis runs over, the one named last changes fastest.
Arguments:
- waves: bfloat16 [256, 131072], P('bands', 'cells'), may hold values from -6 to 6
- stiffness: float32 [125, 125], replicated, as said below
- cell_scale: float32 [8192], P('cells'), may hold values from 0.5 to 4
- potential: float32 [131072], P('cells'), may hold values from -2 to 2
- connect: int32 [125, 8192], P(None, 'cells'), may hold values from 0 to 3071
- live_cells: int32 [64], P('cells'), may hold values from 16 to 128, as said below
- shared: int32 [64, 2, 512], P('cells'), may hold values from 0 to 2047
- window: float32 [2], replicated, may hold values from 1 to 4
Outputs:
- filtered: float32 [256, 131072], P('bands', 'cells')
- projected: float32 [256, 256], P('cells', 'bands')
The draws below stay inside these ranges and needn't reach their ends.
Inputs may be any that keep to these rules, and one draw needn't show every extreme that they name: `live_cells`: at least one partition has all 128 slots live. `stiffness`: symmetric positive definite.
All inputs are finite; a program needn't handle non-finite values.
Results may differ from the reference program's by a relative error of at most 0.0037.
Values may be sent and summed in bfloat16 or wider, within the bound.
No kernel may reach another device: no remote copies, remote signals or barrier semaphores. Data moves between devices by JAX's collectives and lax.ppermute only.
A program may use at most 64 MiB of HBM per device.

```python
import math
import jax
import jax.numpy as jnp
from jax import lax

CELL_NODES = 125
WAVES = 256
NODE_DEV = 2048
GHOST = 512
CELL_CAP = 128
CELLS = 8192
NODES = 131072
N_CELLS = 64


def draw_stiffness(key, part):
    normal_draw = jax.random.normal(key, (CELL_NODES, CELL_NODES), jnp.float32)
    return jnp.dot(normal_draw, normal_draw.T) / CELL_NODES + 0.5 * jnp.eye(CELL_NODES, dtype=jnp.float32)


def draw_live_cells(key, part):
    least = max(1, CELL_CAP // 8)
    counts = jax.random.randint(key, (N_CELLS,), least, CELL_CAP // 2 + 1)
    fullest = jax.random.randint(jax.random.fold_in(key, 7), (), 0, N_CELLS)
    return jnp.where(jnp.arange(N_CELLS) == fullest, CELL_CAP, counts).astype(jnp.int32)


def place_ends(values, key, low, high):
    place = [jax.random.randint(jax.random.fold_in(key, axis), (), 0, length) for axis, length in enumerate(values.shape)]
    longest = values.shape.index(max(values.shape))
    neighbour = place[:longest] + [(place[longest] + 1) % values.shape[longest]] + place[longest + 1:]
    return values.at[tuple(place)].set(low).at[tuple(neighbour)].set(high)


def steps_of(key, dims, pieces, low, top_value):
    def one(axis_at, shards_of):
        heights = jax.random.uniform(jax.random.fold_in(jax.random.fold_in(key, 6), axis_at), (shards_of,), jnp.float32, low / len(pieces), top_value / len(pieces))
        return jnp.repeat(jnp.exp(heights), dims[axis_at] // shards_of).reshape((-1,) + (1,) * (len(dims) - axis_at - 1))

    gain = one(*pieces[0])
    for cut in pieces[1:]:
        gain = gain * one(*cut)
    return gain


def gaussian(rng, shape, scale, limit, shards=(), kind=jnp.bfloat16):
    factor_of = steps_of(rng, shape, shards, -0.22, 0.18) if shards else 1.0
    array = jax.random.normal(rng, shape, jnp.float32) * scale * factor_of
    return jnp.minimum(jnp.maximum(array, -limit), limit).astype(kind)


def setup_inputs(seed: int = 0) -> dict:
    splits = jax.random.split(jax.random.key(seed), 9)
    waves = gaussian(splits[0], (WAVES, NODES), 1.0, 6.0, ((0, 4), (1, 64)))
    stiffness = draw_stiffness(jax.random.fold_in(splits[8], 71), 0)
    cell_scale = jnp.clip(jnp.exp(math.log(4.0) - 2.0794415 * jax.random.uniform(splits[2], (CELLS,), jnp.float32) ** steps_of(splits[2], (CELLS,), ((0, 64),), -0.2, 0.2)), 0.5, 4.0)
    potential = jnp.clip(jax.random.uniform(splits[3], (NODES,), jnp.float32, -2.0, 2.0) * steps_of(splits[3], (NODES,), ((0, 64),), -0.4, 0.0), -2.0, 2.0)
    connect = place_ends(jax.random.randint(splits[4], (CELL_NODES, CELLS), 0, NODE_DEV + 2 * GHOST), jax.random.fold_in(splits[4], 1), 0, (NODE_DEV + 2 * GHOST) - 1).astype(jnp.int32)
    live_cells = draw_live_cells(jax.random.fold_in(splits[8], 71), 0)
    shared = place_ends(jax.random.randint(splits[6], (N_CELLS, 2, GHOST), 0, NODE_DEV), jax.random.fold_in(splits[6], 1), 0, NODE_DEV - 1).astype(jnp.int32)
    window = jnp.clip(jax.random.uniform(splits[7], (2,), jnp.float32, 1.0, 4.0), 1.0, 4.0)
    return dict(waves=waves, stiffness=stiffness, cell_scale=cell_scale, potential=potential, connect=connect, live_cells=live_cells, shared=shared, window=window)


sigma_one = -0.5
sigma_two = 1.0 / (2.0 / sigma_one - sigma_one)


def ghost_blocks(blocks, shared):
    picked = jax.vmap(lambda block_rows, rows_list: block_rows[rows_list])(blocks, shared)
    zeros_block = jnp.zeros((1,) + picked.shape[2:], blocks.dtype)
    lower = jnp.concatenate([zeros_block, picked[:-1, 1]], axis=0)
    upper = jnp.concatenate([picked[1:, 0], zeros_block], axis=0)
    return jnp.concatenate([lower, blocks, upper], axis=1)


def cell_terms(extended, connect, scale, live_count, stiff_rounded):
    columns = extended.shape[1]
    gathered = extended[connect].astype(jnp.float32)
    product = jnp.einsum("ij,cjk->cik", stiff_rounded.astype(jnp.float32), gathered)
    weight = scale * (jnp.arange(connect.shape[0]) < live_count).astype(jnp.float32)
    totals = jnp.zeros((extended.shape[0], columns), jnp.float32)
    return totals.at[connect.reshape(-1)].add((product * weight[:, None, None]).reshape(-1, columns))


def apply_operator(blocks, shared, connect, scale, live_cells, stiff_rounded):
    extended = ghost_blocks(blocks, shared)
    totals = lax.map(lambda items: cell_terms(items[0], items[1], items[2], items[3], stiff_rounded),
                     (extended, connect, scale, live_cells))
    own = totals[:, GHOST:GHOST + NODE_DEV]
    zeros_block = jnp.zeros((1, GHOST, totals.shape[2]), jnp.float32)
    from_lower = jnp.concatenate([zeros_block, totals[:-1, GHOST + NODE_DEV:]], axis=0)
    from_upper = jnp.concatenate([totals[1:, :GHOST], zeros_block], axis=0)
    return jax.vmap(lambda owned, rows_list, lower, upper: owned.at[rows_list[0]].add(lower).at[rows_list[1]].add(upper))(
        own, shared, from_lower, from_upper)


def reference(waves, stiffness, cell_scale, potential, connect, live_cells, shared, window):
    stiff_rounded = stiffness.astype(jnp.bfloat16)
    blocks = waves.T.reshape(N_CELLS, NODE_DEV, WAVES)
    node_pot = potential.reshape(N_CELLS, NODE_DEV, 1)
    cell_conn = connect.T.reshape(N_CELLS, CELL_CAP, CELL_NODES)
    scales = cell_scale.reshape(N_CELLS, CELL_CAP)
    center = window[0]
    half_width = window[1]
    waves32 = blocks.astype(jnp.float32)
    applied_x = apply_operator(blocks, shared, cell_conn, scales, live_cells, stiff_rounded) + node_pot * waves32
    first_pass = ((applied_x - center * waves32) * (sigma_one / half_width)).astype(jnp.bfloat16)
    first32 = first_pass.astype(jnp.float32)
    applied_y = apply_operator(first_pass, shared, cell_conn, scales, live_cells, stiff_rounded) + node_pot * first32
    filtered = (applied_y - center * first32) * (2.0 * sigma_two / half_width) - sigma_one * sigma_two * waves32
    wave_rounded = filtered.astype(jnp.bfloat16)
    applied = apply_operator(wave_rounded, shared, cell_conn, scales, live_cells, stiff_rounded) + node_pot * filtered
    apply_rounded = applied.astype(jnp.bfloat16)
    flat_wave = wave_rounded.reshape(NODES, WAVES)
    flat_apply = apply_rounded.reshape(NODES, WAVES)
    projected = jnp.dot(flat_wave.T, flat_apply, preferred_element_type=jnp.float32) / NODES
    return filtered.reshape(NODES, WAVES).T, projected
```

```python
import jax
import jax.numpy as jnp
from jax import lax
from jax.experimental import pallas as pl
from jax.experimental.pallas import tpu as pltpu
from jax.sharding import PartitionSpec as P

sigma_one = -0.5
sigma_two = 1.0 / (2.0 / sigma_one - sigma_one)

LANES = 128
HALF = 64
GROUP = 8
PAIRS = GROUP // 2
STEP = 25

VMEM = pl.BlockSpec(memory_space=pltpu.VMEM)
SMEM = pl.BlockSpec(memory_space=pltpu.SMEM)
PARAMS = pltpu.CompilerParams(vmem_limit_bytes=56 << 20)
f32 = jnp.float32
bf16 = jnp.bfloat16


def shape_of(rows, lanes, dtype):
    return jax.ShapeDtypeStruct((rows, lanes), dtype)


def left_lanes():
    return lax.broadcasted_iota(jnp.int32, (1, LANES), 1) < HALF


def swap(x):
    return pltpu.roll(x, HALF, 1)


def pack(rows):
    half = rows.shape[0] // 2
    return jnp.where(left_lanes(), rows[:half], rows[half:])


def unpack(x):
    left = left_lanes()
    other = swap(x)
    return jnp.where(left, x, other), jnp.where(left, other, x)


def pick_rows(values, shared_ref, base, count, stage):
    left = left_lanes()

    def some(turn, carry):
        for step in range(8):
            k = turn * 8 + step
            one = values[pl.ds(shared_ref[base + k], 1), :]
            two = values[pl.ds(shared_ref[base + count + k], 1), :]
            stage[pl.ds(k, 1), :] = jnp.where(left, one, two)
        return carry

    lax.fori_loop(0, count // 8, some, 0)


def send_lists(values, shared_ref, low_ref, high_ref, stage):
    count = stage.shape[0]
    pick_rows(values, shared_ref, 0, count, stage)
    low_ref[...] = stage[...].astype(bf16)
    pick_rows(values, shared_ref, 2 * count, count, stage)
    high_ref[...] = stage[...].astype(bf16)


def prepare_kernel(shared_ref, waves_ref, rows_ref, low_ref, high_ref, stage):
    block = waves_ref[...].astype(f32)
    rows_ref[...] = jnp.transpose(jnp.concatenate([block, block], axis=0))
    send_lists(rows_ref, shared_ref, low_ref, high_ref, stage)


def cell_sums(live_ref, index_ref, scale_ref, stiff_ref, own_ref, low_ref, high_ref, x, g, p, acc):
    left = left_lanes()
    ghost = 2 * low_ref.shape[0]
    half = ghost // 2
    owned = own_ref.shape[0]
    nodes = 125
    capacity = scale_ref.shape[0]
    x[pl.ds(ghost, owned), :] = own_ref[...]
    for first, ref in ((0, low_ref), (ghost + owned, high_ref)):
        one, two = unpack(ref[...].astype(f32))
        x[pl.ds(first, half), :] = one
        x[pl.ds(first + half, half), :] = two
    for a in acc:
        a[...] = jnp.zeros_like(a)
    for q in range(PAIRS):
        g[q, 120:128, :] = jnp.zeros((8, LANES), f32)
    live = live_ref[0]

    def gather(i, base):
        for q in range(PAIRS):
            one = x[pl.ds(index_ref[base + i * capacity + 2 * q], 1), :]
            two = x[pl.ds(index_ref[base + i * capacity + 2 * q + 1], 1), :]
            g[q, pl.ds(i, 1), :] = jnp.where(left, one, two)

    def scatter(i, base):
        rows = [p[q, pl.ds(i, 1), :] for q in range(PAIRS)]
        for k in range(GROUP):
            acc[k][pl.ds(index_ref[base + i * capacity + k], 1), :] += rows[k // 2]

    def each_row(f):
        def some(turn, carry):
            for step in range(STEP):
                f(turn * STEP + step)
            return carry

        lax.fori_loop(0, nodes // STEP, some, 0)

    each_row(lambda i: gather(i, 0))
    stiff = stiff_ref[...]

    def one_group(turn, carry):
        base = turn * GROUP
        following = jnp.minimum(turn + 1, capacity // GROUP - 1) * GROUP
        for q in range(0, PAIRS, 2):
            both = jnp.concatenate([g[q].astype(bf16), g[q + 1].astype(bf16)], axis=1)
            product = jnp.dot(stiff, both, preferred_element_type=f32)
            for h in range(2):
                cell = base + 2 * (q + h)
                one = jnp.where(cell < live, scale_ref[cell], 0.0)
                two = jnp.where(cell + 1 < live, scale_ref[cell + 1], 0.0)
                p[q + h] = product[:, h * LANES : (h + 1) * LANES] * jnp.where(left, one, two)

        def step(i):
            scatter(i, base)
            gather(i, following)

        each_row(step)
        return carry

    lax.fori_loop(0, (live + GROUP - 1) // GROUP, one_group, 0)

    def total(first, count):
        one = acc[0][pl.ds(first, count), :]
        two = acc[1][pl.ds(first, count), :]
        for q in range(1, PAIRS):
            one = one + acc[2 * q][pl.ds(first, count), :]
            two = two + acc[2 * q + 1][pl.ds(first, count), :]
        both = jnp.where(left, one, two)
        return both + swap(both)

    return total


def cells_kernel(
    live_ref, index_ref, scale_ref, stiff_ref, own_ref, low_ref, high_ref,
    sums_ref, sums_low_ref, sums_high_ref, x, g, p, *acc
):
    total = cell_sums(live_ref, index_ref, scale_ref, stiff_ref, own_ref, low_ref, high_ref, x, g, p, acc)
    ghost = 2 * low_ref.shape[0]
    owned = own_ref.shape[0]
    sums_ref[...] = total(ghost, owned)
    sums_low_ref[...] = pack(total(0, ghost))
    sums_high_ref[...] = pack(total(ghost + owned, ghost))


def last_cells_kernel(
    live_ref, index_ref, scale_ref, stiff_ref, own_ref, low_ref, high_ref, local_ref,
    packed_ref, x, g, p, *acc
):
    total = cell_sums(live_ref, index_ref, scale_ref, stiff_ref, own_ref, low_ref, high_ref, x, g, p, acc)
    ghost = 2 * low_ref.shape[0]
    owned = own_ref.shape[0]
    half = ghost // 2
    packed_ref[pl.ds(0, half), :] = pack(total(0, ghost))
    for m in range(owned // ghost):
        part = total(ghost + m * ghost, ghost) + local_ref[pl.ds(m * ghost, ghost), :]
        packed_ref[pl.ds(half + m * half, half), :] = pack(part)
    packed_ref[pl.ds(half + owned // 2, half), :] = pack(total(ghost + owned, ghost))


def assembled(shared_ref, sums_ref, lower_ref, upper_ref, acc):
    left = left_lanes()
    count = lower_ref.shape[0]
    for a in acc:
        a[...] = jnp.zeros_like(a)

    def some(turn, carry):
        for step in range(8):
            k = turn * 8 + step
            for side, ref in ((0, lower_ref), (1, upper_ref)):
                row = ref[pl.ds(k, 1), :]
                for part in range(2):
                    at = shared_ref[2 * count * side + count * part + k]
                    acc[2 * side + part][pl.ds(at, 1), :] += row
        return carry

    lax.fori_loop(0, count // 8, some, 0)
    both = jnp.where(left, acc[0][...] + acc[2][...], acc[1][...] + acc[3][...])
    return sums_ref[...] + (both + swap(both))


def first_kernel(
    shared_ref, window_ref, sums_ref, lower_ref, upper_ref, waves_ref, potential_ref,
    rows_ref, low_ref, high_ref, stage, *acc
):
    waves = waves_ref[...]
    applied = assembled(shared_ref, sums_ref, lower_ref, upper_ref, acc) + potential_ref[...] * waves
    first = (applied - window_ref[0] * waves) * window_ref[1]
    rows_ref[...] = first.astype(bf16).astype(f32)
    send_lists(rows_ref, shared_ref, low_ref, high_ref, stage)


def second_kernel(
    shared_ref, window_ref, sums_ref, lower_ref, upper_ref, waves_ref, first_ref, potential_ref,
    rows_ref, low_ref, high_ref, packed_ref, local_ref, filtered_ref, stage, *acc
):
    first = first_ref[...]
    potential = potential_ref[...]
    applied = assembled(shared_ref, sums_ref, lower_ref, upper_ref, acc) + potential * first
    filtered = (applied - window_ref[0] * first) * window_ref[2] - (sigma_one * sigma_two) * waves_ref[...]
    rounded = filtered.astype(bf16).astype(f32)
    rows_ref[...] = rounded
    send_lists(rows_ref, shared_ref, low_ref, high_ref, stage)
    local_ref[...] = potential * filtered
    half = low_ref.shape[0]
    for m in range(rounded.shape[0] // (2 * half)):
        part = pack(rounded[2 * half * m : 2 * half * (m + 1)])
        packed_ref[pl.ds(half * m, half), :] = part.astype(bf16)
    filtered_ref[...] = jnp.transpose(filtered)[:HALF]


def product_kernel(band_ref, sums_ref, *refs):
    parts, (out_ref, product) = refs[:-2], refs[-2:]
    turned = jnp.transpose(sums_ref[...])
    coarse = turned.astype(bf16)
    fine = (turned - coarse.astype(f32)).astype(bf16)
    left_side = jnp.concatenate([coarse, fine], axis=0)
    bands = len(parts) // 3
    for shift in range(bands):
        at = lax.rem(band_ref[0] + shift, bands) * HALF
        block = jnp.concatenate([ref[...] for ref in parts[3 * shift : 3 * shift + 3]], axis=0)
        both = jnp.dot(left_side, block, preferred_element_type=f32)
        both = both[:LANES] + both[LANES:]
        square = jnp.transpose(both + swap(pltpu.roll(both, HALF, 0)))
        product[pl.ds(pl.multiple_of(at, HALF), HALF), :] = square[:HALF]
    left = left_lanes()
    chunks = product.shape[0] // 4
    four = [product[pl.ds(r, chunks, stride=4), :] for r in range(4)]
    out_ref[:, 0:LANES] = jnp.where(left, four[0], swap(four[1]))
    out_ref[:, LANES : 2 * LANES] = jnp.where(left, four[2], swap(four[3]))


def local(waves, stiffness, cell_scale, potential, connect, live_cells, shared, window):
    columns, owned = waves.shape
    ghost = shared.shape[2]
    half = ghost // 2
    extended = owned + 2 * ghost
    nodes = connect.shape[0]
    cell_count = lax.axis_size("cells")
    band_count = lax.axis_size("bands")
    shared_list = shared.reshape(-1)
    index = connect.reshape(-1)
    stiff = jnp.pad(stiffness.astype(bf16), ((0, LANES - nodes), (0, LANES - nodes)))
    numbers = jnp.stack([window[0], sigma_one / window[1], 2.0 * sigma_two / window[1]])
    potential_rows = jnp.broadcast_to(potential[:, None], (owned, LANES))
    forward = [(i, i + 1) for i in range(cell_count - 1)]
    backward = [(target, source) for source, target in forward]

    def exchange(low, high):
        return lax.ppermute(high, "cells", forward), lax.ppermute(low, "cells", backward)

    rows_of = shape_of(owned, LANES, f32)
    list_of = shape_of(half, LANES, bf16)
    stage_of = pltpu.VMEM((half, LANES), f32)
    cell_scratch = [
        pltpu.VMEM((extended, LANES), f32),
        pltpu.VMEM((PAIRS, LANES, LANES), f32),
        pltpu.VMEM((PAIRS, LANES, LANES), f32),
    ] + [pltpu.VMEM((extended, LANES), f32)] * GROUP
    node_scratch = [stage_of] + [pltpu.VMEM((owned, LANES), f32)] * 4

    def call(kernel, outs, scratch, smem, vmem, name):
        return pl.pallas_call(
            kernel,
            out_shape=outs,
            in_specs=[SMEM] * len(smem) + [VMEM] * len(vmem),
            out_specs=jax.tree.map(lambda _: VMEM, outs),
            scratch_shapes=scratch,
            compiler_params=PARAMS,
            name=name,
        )(*smem, *vmem)

    waves_rows, low, high = call(
        prepare_kernel, (rows_of, list_of, list_of), [stage_of], (shared_list,), (waves,), "prepare"
    )
    tables = (live_cells, index, cell_scale)
    edge_of = shape_of(half, LANES, f32)

    def cells(rows, below, above):
        sums, sums_low, sums_high = call(
            cells_kernel, (rows_of, edge_of, edge_of), cell_scratch, tables, (stiff, rows, below, above), "cells"
        )
        lower, upper = exchange(sums_low, sums_high)
        return sums, lower, upper

    below, above = exchange(low, high)
    sums, lower, upper = cells(waves_rows, below, above)
    first_rows, low, high = call(
        first_kernel, (rows_of, list_of, list_of), node_scratch, (shared_list, numbers),
        (sums, lower, upper, waves_rows, potential_rows), "first",
    )
    below, above = exchange(low, high)
    sums, lower, upper = cells(first_rows, below, above)
    rounded_rows, low, high, packed, local_rows, filtered = call(
        second_kernel,
        (rows_of, list_of, list_of, shape_of(owned // 2, LANES, bf16), rows_of, shape_of(columns, owned, f32)),
        node_scratch, (shared_list, numbers),
        (sums, lower, upper, waves_rows, first_rows, potential_rows), "second",
    )
    below, above = exchange(low, high)
    parts = [below, packed, above]
    for shift in range(1, band_count):
        turn = [((b + shift) % band_count, b) for b in range(band_count)]
        parts += [lax.ppermute(part, "bands", turn) for part in (below, packed, above)]
    packed_sums = call(
        last_cells_kernel, shape_of(extended // 2, LANES, f32), cell_scratch, tables,
        (stiff, rounded_rows, below, above, local_rows), "last_cells",
    )
    band = lax.axis_index("bands").reshape(1).astype(jnp.int32)
    waves_all = columns * band_count
    partial_value = call(
        product_kernel, shape_of(waves_all // 4, 4 * HALF, f32),
        [pltpu.VMEM((waves_all, LANES), f32)], (band,), (packed_sums, *parts), "product",
    )
    arrived = lax.all_to_all(partial_value, "cells", split_axis=0, concat_axis=0, tiled=True)
    own_rows = waves_all // cell_count
    projected = (arrived.sum(axis=0) * (1.0 / (owned * cell_count))).reshape(own_rows, columns)
    return (filtered, projected)


def solution(mesh):
    return jax.shard_map(
        local,
        mesh=mesh,
        in_specs=(
            P("bands", "cells"),
            P(),
            P("cells"),
            P("cells"),
            P(None, "cells"),
            P("cells"),
            P("cells", None, None),
            P(),
        ),
        out_specs=(P("bands", "cells"), P("cells", "bands")),
        check_vma=False,
    )
```

```python
import jax
import jax.numpy as jnp
from jax import lax
from jax.experimental import pallas as pl
from jax.experimental.pallas import tpu as pltpu
from jax.sharding import PartitionSpec as P

sigma_one = -0.5
sigma_two = 1.0 / (2.0 / sigma_one - sigma_one)


LANES = 128
HALF = 64
GROUP = 8
PAIRS = GROUP // 2
NODES = 125

VMEM = pl.BlockSpec(memory_space=pltpu.VMEM)
SMEM = pl.BlockSpec(memory_space=pltpu.SMEM)
PLACED = pl.BlockSpec(memory_space=pl.ANY)
f32 = jnp.float32
bf16 = jnp.bfloat16


def shape_of(rows, lanes, dtype):
    return jax.ShapeDtypeStruct((rows, lanes), dtype)


def left_lanes():
    return lax.broadcasted_iota(jnp.int32, (1, LANES), 1) < HALF


def swap(x):
    return pltpu.roll(x, HALF, 1)


def pack(rows):
    half = rows.shape[0] // 2
    return jnp.where(left_lanes(), rows[:half], rows[half:])


def unpack(x):
    left = left_lanes()
    other = swap(x)
    return jnp.where(left, x, other), jnp.where(left, other, x)


def pick_rows(values, shared_ref, base, count, stage):
    left = left_lanes()

    def some(turn, carry):
        for step in range(8):
            k = turn * 8 + step
            one = values[pl.ds(shared_ref[base + k], 1), :]
            two = values[pl.ds(shared_ref[base + count + k], 1), :]
            stage[pl.ds(k, 1), :] = jnp.where(left, one, two)
        return carry

    lax.fori_loop(0, count // 8, some, 0)


def send_lists(values, shared_ref, low_ref, high_ref, stage):
    count = stage.shape[0]
    pick_rows(values, shared_ref, 0, count, stage)
    low_ref[...] = stage[...].astype(bf16)
    pick_rows(values, shared_ref, 2 * count, count, stage)
    high_ref[...] = stage[...].astype(bf16)


def prepare_kernel(shared_ref, waves_ref, rows_ref, low_ref, high_ref, stage):
    block = waves_ref[...].astype(f32)
    rows_ref[...] = jnp.transpose(jnp.concatenate([block, block], axis=0))
    send_lists(rows_ref, shared_ref, low_ref, high_ref, stage)


def cell_sums(live_ref, scale_ref, index_ref, stiff_ref, own_ref, low_ref, high_ref, even, odd, sems, x, g, p, acc):
    left = left_lanes()
    ghost = 2 * low_ref.shape[0]
    half = ghost // 2
    owned = own_ref.shape[0]
    groups = scale_ref.shape[0] // GROUP
    size = even.shape[0]

    def fetch(group, slot, n):
        first = pl.multiple_of(jnp.minimum(group, groups - 1) * size, size)
        return pltpu.make_async_copy(index_ref.at[pl.ds(first, size)], slot, sems.at[n])

    fetch(0, even, 0).start()
    fetch(1, odd, 1).start()
    x[pl.ds(ghost, owned), :] = own_ref[...]
    for first, ref in ((0, low_ref), (ghost + owned, high_ref)):
        one, two = unpack(ref[...].astype(f32))
        x[pl.ds(first, half), :] = one
        x[pl.ds(first + half, half), :] = two
    for a in acc:
        a[...] = jnp.zeros_like(a)
    for q in range(PAIRS):
        g[q, 120:128, :] = jnp.zeros((8, LANES), f32)
    live = live_ref[0]
    stiff = stiff_ref[...]

    def one_group(group, slot):
        base = group * GROUP
        for i in range(NODES):
            for q in range(PAIRS):
                one = x[pl.ds(slot[2 * q * LANES + i], 1), :]
                two = x[pl.ds(slot[(2 * q + 1) * LANES + i], 1), :]
                g[q, pl.ds(i, 1), :] = jnp.where(left, one, two)
        for q in range(0, PAIRS, 2):
            both = jnp.concatenate([g[q].astype(bf16), g[q + 1].astype(bf16)], axis=1)
            product = jnp.dot(stiff, both, preferred_element_type=f32)
            for h in range(2):
                cell = base + 2 * (q + h)
                one = jnp.where(cell < live, scale_ref[cell], 0.0)
                two = jnp.where(cell + 1 < live, scale_ref[cell + 1], 0.0)
                p[q + h] = product[:, h * LANES : (h + 1) * LANES] * jnp.where(left, one, two)
        for i in range(NODES):
            rows = [p[q, pl.ds(i, 1), :] for q in range(PAIRS)]
            for k in range(GROUP):
                acc[k][pl.ds(slot[k * LANES + i], 1), :] += rows[k // 2]

    def two_groups(turn, carry):
        fetch(2 * turn, even, 0).wait()
        one_group(2 * turn, even)
        fetch(2 * turn + 2, even, 0).start()
        fetch(2 * turn + 1, odd, 1).wait()
        one_group(2 * turn + 1, odd)
        fetch(2 * turn + 3, odd, 1).start()
        return carry

    lax.fori_loop(0, (live + 2 * GROUP - 1) // (2 * GROUP), two_groups, 0)
    fetch(0, even, 0).wait()
    fetch(0, odd, 1).wait()

    def total(first, count):
        one = acc[0][pl.ds(first, count), :]
        two = acc[1][pl.ds(first, count), :]
        for q in range(1, PAIRS):
            one = one + acc[2 * q][pl.ds(first, count), :]
            two = two + acc[2 * q + 1][pl.ds(first, count), :]
        both = jnp.where(left, one, two)
        return both + swap(both)

    return total


def cells_kernel(
    live_ref, scale_ref, index_ref, stiff_ref, own_ref, low_ref, high_ref,
    sums_ref, sums_low_ref, sums_high_ref, even, odd, sems, x, g, p, *acc
):
    total = cell_sums(
        live_ref, scale_ref, index_ref, stiff_ref, own_ref, low_ref, high_ref, even, odd, sems, x, g, p, acc
    )
    ghost = 2 * low_ref.shape[0]
    owned = own_ref.shape[0]
    sums_ref[...] = total(ghost, owned)
    sums_low_ref[...] = pack(total(0, ghost))
    sums_high_ref[...] = pack(total(ghost + owned, ghost))


def last_cells_kernel(
    live_ref, scale_ref, index_ref, stiff_ref, own_ref, low_ref, high_ref, local_ref,
    packed_ref, even, odd, sems, x, g, p, *acc
):
    total = cell_sums(
        live_ref, scale_ref, index_ref, stiff_ref, own_ref, low_ref, high_ref, even, odd, sems, x, g, p, acc
    )
    ghost = 2 * low_ref.shape[0]
    owned = own_ref.shape[0]
    half = ghost // 2
    packed_ref[pl.ds(0, half), :] = pack(total(0, ghost))
    for m in range(owned // ghost):
        part = total(ghost + m * ghost, ghost) + local_ref[pl.ds(m * ghost, ghost), :]
        packed_ref[pl.ds(half + m * half, half), :] = pack(part)
    packed_ref[pl.ds(half + owned // 2, half), :] = pack(total(ghost + owned, ghost))


def assembled(shared_ref, sums_ref, lower_ref, upper_ref, acc):
    left = left_lanes()
    count = lower_ref.shape[0]
    for a in acc:
        a[...] = jnp.zeros_like(a)

    def some(turn, carry):
        for step in range(8):
            k = turn * 8 + step
            for side, ref in ((0, lower_ref), (1, upper_ref)):
                row = ref[pl.ds(k, 1), :]
                for part in range(2):
                    at = shared_ref[2 * count * side + count * part + k]
                    acc[2 * side + part][pl.ds(at, 1), :] += row
        return carry

    lax.fori_loop(0, count // 8, some, 0)
    both = jnp.where(left, acc[0][...] + acc[2][...], acc[1][...] + acc[3][...])
    return sums_ref[...] + (both + swap(both))


def first_kernel(
    shared_ref, window_ref, sums_ref, lower_ref, upper_ref, waves_ref, potential_ref,
    rows_ref, low_ref, high_ref, stage, *acc
):
    waves = waves_ref[...]
    applied = assembled(shared_ref, sums_ref, lower_ref, upper_ref, acc) + potential_ref[...] * waves
    first = (applied - window_ref[0] * waves) * (sigma_one / jnp.full((1, LANES), window_ref[1], f32))
    rows_ref[...] = first.astype(bf16).astype(f32)
    send_lists(rows_ref, shared_ref, low_ref, high_ref, stage)


def second_kernel(
    shared_ref, window_ref, sums_ref, lower_ref, upper_ref, waves_ref, first_ref, potential_ref,
    rows_ref, low_ref, high_ref, packed_ref, local_ref, filtered_ref, stage, *acc
):
    first = first_ref[...]
    potential = potential_ref[...]
    applied = assembled(shared_ref, sums_ref, lower_ref, upper_ref, acc) + potential * first
    gain = 2.0 * sigma_two / jnp.full((1, LANES), window_ref[1], f32)
    filtered = (applied - window_ref[0] * first) * gain - (sigma_one * sigma_two) * waves_ref[...]
    rounded = filtered.astype(bf16).astype(f32)
    rows_ref[...] = rounded
    send_lists(rows_ref, shared_ref, low_ref, high_ref, stage)
    local_ref[...] = potential * filtered
    half = low_ref.shape[0]
    for m in range(rounded.shape[0] // (2 * half)):
        part = pack(rounded[2 * half * m : 2 * half * (m + 1)])
        packed_ref[pl.ds(half * (m + 1), half), :] = part.astype(bf16)
    filtered_ref[...] = jnp.transpose(filtered)[:HALF]


def product_kernel(band_ref, sums_ref, *refs):
    parts, (out_ref, product) = refs[:-2], refs[-2:]
    turned = jnp.transpose(sums_ref[...])
    coarse = turned.astype(bf16)
    fine = (turned - coarse.astype(f32)).astype(bf16)
    left_side = jnp.concatenate([coarse, fine], axis=0)
    bands = len(parts)
    for shift in range(bands):
        at = lax.rem(band_ref[0] + shift, bands) * HALF
        both = jnp.dot(left_side, parts[shift][...], preferred_element_type=f32)
        both = both[:LANES] + both[LANES:]
        square = jnp.transpose(both + swap(pltpu.roll(both, HALF, 0)))
        product[pl.ds(pl.multiple_of(at, HALF), HALF), :] = square[:HALF]
    left = left_lanes()
    chunks = product.shape[0] // 4
    four = [product[pl.ds(r, chunks, stride=4), :] for r in range(4)]
    out_ref[:, 0:LANES] = jnp.where(left, four[0], swap(four[1]))
    out_ref[:, LANES : 2 * LANES] = jnp.where(left, four[2], swap(four[3]))


def local(waves, stiffness, cell_scale, potential, connect, live_cells, shared, window):
    columns, owned = waves.shape
    ghost = shared.shape[2]
    half = ghost // 2
    extended = owned + 2 * ghost
    nodes = connect.shape[0]
    cell_count = lax.axis_size("cells")
    band_count = lax.axis_size("bands")
    shared_list = shared.reshape(-1)
    index = jnp.pad(connect.T, ((0, 0), (0, LANES - nodes))).reshape(-1)
    stiff = jnp.pad(stiffness.astype(bf16), ((0, LANES - nodes), (0, LANES - nodes)))
    potential_rows = jnp.broadcast_to(potential[:, None], (owned, LANES))
    forward = [(i, i + 1) for i in range(cell_count - 1)]
    backward = [(target, source) for source, target in forward]

    def exchange(low, high):
        return lax.ppermute(high, "cells", forward), lax.ppermute(low, "cells", backward)

    rows_of = shape_of(owned, LANES, f32)
    list_of = shape_of(half, LANES, bf16)
    stage_of = pltpu.VMEM((half, LANES), f32)
    cell_scratch = [
        pltpu.SMEM((GROUP * LANES,), jnp.int32),
        pltpu.SMEM((GROUP * LANES,), jnp.int32),
        pltpu.SemaphoreType.DMA((2,)),
        pltpu.VMEM((extended, LANES), f32),
        pltpu.VMEM((PAIRS, LANES, LANES), f32),
        pltpu.VMEM((PAIRS, LANES, LANES), f32),
    ] + [pltpu.VMEM((extended, LANES), f32)] * GROUP
    node_scratch = [stage_of] + [pltpu.VMEM((owned, LANES), f32)] * 4

    def call(kernel, outs, scratch, smem, vmem, name, placed=(), limit=10, flops=0):
        return pl.pallas_call(
            kernel,
            out_shape=outs,
            in_specs=[SMEM] * len(smem) + [PLACED] * len(placed) + [VMEM] * len(vmem),
            out_specs=jax.tree.map(lambda _: VMEM, outs),
            scratch_shapes=scratch,
            compiler_params=pltpu.CompilerParams(vmem_limit_bytes=limit << 20),
            cost_estimate=pl.CostEstimate(flops=flops, transcendentals=0, bytes_accessed=4 << 20),
            name=name,
        )(*smem, *placed, *vmem)

    waves_rows, low, high = call(
        prepare_kernel, (rows_of, list_of, list_of), [stage_of], (shared_list,), (waves,), "prepare"
    )
    tables = (live_cells, cell_scale)
    work = dict(placed=(index,), limit=18, flops=20 * 10**9)
    edge_of = shape_of(half, LANES, f32)

    def cells(rows, below, above):
        sums, sums_low, sums_high = call(
            cells_kernel, (rows_of, edge_of, edge_of), cell_scratch, tables, (stiff, rows, below, above), "cells", **work
        )
        lower, upper = exchange(sums_low, sums_high)
        return sums, lower, upper

    below, above = exchange(low, high)
    sums, lower, upper = cells(waves_rows, below, above)
    first_rows, low, high = call(
        first_kernel, (rows_of, list_of, list_of), node_scratch, (shared_list, window),
        (sums, lower, upper, waves_rows, potential_rows), "first",
    )
    below, above = exchange(low, high)
    sums, lower, upper = cells(first_rows, below, above)
    rounded_rows, low, high, packed, local_rows, filtered = call(
        second_kernel,
        (rows_of, list_of, list_of, shape_of(extended // 2, LANES, bf16), rows_of, shape_of(columns, owned, f32)),
        node_scratch, (shared_list, window),
        (sums, lower, upper, waves_rows, first_rows, potential_rows), "second",
    )
    below, above = exchange(low, high)
    packed = lax.dynamic_update_slice(packed, below, (0, 0))
    packed = lax.dynamic_update_slice(packed, above, (half + owned // 2, 0))
    parts = [packed]
    for shift in range(1, band_count):
        turn = [((b + shift) % band_count, b) for b in range(band_count)]
        parts.append(lax.ppermute(packed, "bands", turn))
    packed_sums = call(
        last_cells_kernel, shape_of(extended // 2, LANES, f32), cell_scratch, tables,
        (stiff, rounded_rows, below, above, local_rows), "last_cells", **work,
    )
    band = lax.axis_index("bands").reshape(1).astype(jnp.int32)
    waves_all = columns * band_count
    partial_value = call(
        product_kernel, shape_of(waves_all // 4, 4 * HALF, f32),
        [pltpu.VMEM((waves_all, LANES), f32)], (band,), (packed_sums, *parts), "product",
    )
    arrived = lax.all_to_all(partial_value, "cells", split_axis=0, concat_axis=0, tiled=True)
    own_rows = waves_all // cell_count
    projected = (arrived.sum(axis=0) * (1.0 / (owned * cell_count))).reshape(own_rows, columns)
    return (filtered, projected)


def solution(mesh):
    return jax.shard_map(
        local,
        mesh=mesh,
        in_specs=(
            P("bands", "cells"),
            P(),
            P("cells"),
            P("cells"),
            P(None, "cells"),
            P("cells"),
            P("cells", None, None),
            P(),
        ),
        out_specs=(P("bands", "cells"), P("cells", "bands")),
        check_vma=False,
    )
```

```python
import jax
import jax.numpy as jnp
from jax import lax
from jax.experimental import pallas as pl
from jax.experimental.pallas import tpu as pltpu
from jax.sharding import PartitionSpec as P

sigma_one = -0.5
sigma_two = 1.0 / (2.0 / sigma_one - sigma_one)


LANES = 128
HALF = 64
GROUP = 8
PAIRS = GROUP // 2
NODES = 125

VMEM = pl.BlockSpec(memory_space=pltpu.VMEM)
SMEM = pl.BlockSpec(memory_space=pltpu.SMEM)
PLACED = pl.BlockSpec(memory_space=pl.ANY)
f32 = jnp.float32
bf16 = jnp.bfloat16


def shape_of(rows, lanes, dtype):
    return jax.ShapeDtypeStruct((rows, lanes), dtype)


def left_lanes():
    return lax.broadcasted_iota(jnp.int32, (1, LANES), 1) < HALF


def swap(x):
    return pltpu.roll(x, HALF, 1)


def pack(rows):
    half = rows.shape[0] // 2
    return jnp.where(left_lanes(), rows[:half], rows[half:])


def unpack(x):
    left = left_lanes()
    other = swap(x)
    return jnp.where(left, x, other), jnp.where(left, other, x)


def pick_rows(values, shared_ref, base, count, stage):
    left = left_lanes()

    def some(turn, carry):
        for step in range(8):
            k = turn * 8 + step
            one = values[pl.ds(shared_ref[base + k], 1), :]
            two = values[pl.ds(shared_ref[base + count + k], 1), :]
            stage[pl.ds(k, 1), :] = jnp.where(left, one, two)
        return carry

    lax.fori_loop(0, count // 8, some, 0)


def bases(odd_ref, size):
    return size * (1 - odd_ref[0]), size * odd_ref[0]


def send_lists(values, odd_ref, shared_ref, a_ref, b_ref, stage):
    count = stage.shape[0]
    for base, ref in zip(bases(odd_ref, 2 * count), (a_ref, b_ref)):
        pick_rows(values, shared_ref, base, count, stage)
        ref[...] = stage[...].astype(bf16)


def prepare_kernel(odd_ref, shared_ref, waves_ref, rows_ref, a_ref, b_ref, stage):
    block = waves_ref[...].astype(f32)
    rows_ref[...] = jnp.transpose(jnp.concatenate([block, block], axis=0))
    send_lists(rows_ref, odd_ref, shared_ref, a_ref, b_ref, stage)


def cell_sums(odd_ref, live_ref, scale_ref, index_ref, stiff_ref, own_ref, a_ref, b_ref, even, odd, sems, x, g, p, acc):
    left = left_lanes()
    half = a_ref.shape[0]
    ghost = 2 * half
    owned = own_ref.shape[0]
    groups = scale_ref.shape[0] // GROUP
    size = even.shape[0]

    def fetch(group, slot, n):
        first = pl.multiple_of(jnp.minimum(group, groups - 1) * size, size)
        return pltpu.make_async_copy(index_ref.at[pl.ds(first, size)], slot, sems.at[n])

    fetch(0, even, 0).start()
    fetch(1, odd, 1).start()
    x[pl.ds(ghost, owned), :] = own_ref[...]
    edges = [pl.multiple_of(first, 8) for first in bases(odd_ref, ghost + owned)]
    for first, ref in zip(edges, (a_ref, b_ref)):
        one, two = unpack(ref[...].astype(f32))
        x[pl.ds(first, half), :] = one
        x[pl.ds(first + half, half), :] = two
    for a in acc:
        a[...] = jnp.zeros_like(a)
    for q in range(PAIRS):
        g[q, 120:128, :] = jnp.zeros((8, LANES), f32)
    live = live_ref[0]
    stiff = stiff_ref[...]

    def one_group(group, slot):
        base = group * GROUP
        for i in range(NODES):
            for q in range(PAIRS):
                one = x[pl.ds(slot[2 * q * LANES + i], 1), :]
                two = x[pl.ds(slot[(2 * q + 1) * LANES + i], 1), :]
                g[q, pl.ds(i, 1), :] = jnp.where(left, one, two)
        for q in range(0, PAIRS, 2):
            both = jnp.concatenate([g[q].astype(bf16), g[q + 1].astype(bf16)], axis=1)
            product = jnp.dot(stiff, both, preferred_element_type=f32)
            for h in range(2):
                cell = base + 2 * (q + h)
                one = jnp.where(cell < live, scale_ref[cell], 0.0)
                two = jnp.where(cell + 1 < live, scale_ref[cell + 1], 0.0)
                p[q + h] = product[:, h * LANES : (h + 1) * LANES] * jnp.where(left, one, two)
        for i in range(NODES):
            rows = [p[q, pl.ds(i, 1), :] for q in range(PAIRS)]
            for k in range(GROUP):
                acc[k][pl.ds(slot[k * LANES + i], 1), :] += rows[k // 2]

    def two_groups(turn, carry):
        fetch(2 * turn, even, 0).wait()
        one_group(2 * turn, even)
        fetch(2 * turn + 2, even, 0).start()
        fetch(2 * turn + 1, odd, 1).wait()
        one_group(2 * turn + 1, odd)
        fetch(2 * turn + 3, odd, 1).start()
        return carry

    lax.fori_loop(0, (live + 2 * GROUP - 1) // (2 * GROUP), two_groups, 0)
    fetch(0, even, 0).wait()
    fetch(0, odd, 1).wait()

    def total(first, count):
        one = acc[0][pl.ds(first, count), :]
        two = acc[1][pl.ds(first, count), :]
        for q in range(1, PAIRS):
            one = one + acc[2 * q][pl.ds(first, count), :]
            two = two + acc[2 * q + 1][pl.ds(first, count), :]
        both = jnp.where(left, one, two)
        return both + swap(both)

    return total(ghost, owned), *(pack(total(first, ghost)) for first in edges)


def cells_kernel(*refs):
    ins, (sums_ref, a_ref, b_ref), scratch = refs[:8], refs[8:11], refs[11:]
    sums_ref[...], a_ref[...], b_ref[...] = cell_sums(*ins, *scratch[:6], scratch[6:])


def last_cells_kernel(*refs):
    ins, packed_ref, scratch = refs[:8], refs[8], refs[9:]
    sums, a_part, b_part = cell_sums(*ins, *scratch[:6], scratch[6:])
    half = a_part.shape[0]
    own = sums.shape[0] // 2
    packed_ref[pl.ds(0, half), :] = a_part
    for m in range(own // half):
        packed_ref[pl.ds(half + m * half, half), :] = pack(sums[2 * half * m : 2 * half * (m + 1)])
    packed_ref[pl.ds(half + own, half), :] = b_part


def assembled(odd_ref, shared_ref, sums_ref, a_ref, b_ref, acc):
    left = left_lanes()
    count = a_ref.shape[0]
    sides = tuple(zip(bases(odd_ref, 2 * count), (a_ref, b_ref)))
    for a in acc:
        a[...] = jnp.zeros_like(a)

    def some(turn, carry):
        for step in range(8):
            k = turn * 8 + step
            for side, (base, ref) in enumerate(sides):
                row = ref[pl.ds(k, 1), :]
                for part in range(2):
                    at = shared_ref[base + count * part + k]
                    acc[2 * side + part][pl.ds(at, 1), :] += row
        return carry

    lax.fori_loop(0, count // 8, some, 0)
    both = jnp.where(left, acc[0][...] + acc[2][...], acc[1][...] + acc[3][...])
    return sums_ref[...] + (both + swap(both))


def first_kernel(
    odd_ref, shared_ref, window_ref, sums_ref, from_a_ref, from_b_ref, waves_ref, potential_ref,
    rows_ref, a_ref, b_ref, stage, *acc
):
    waves = waves_ref[...]
    applied = assembled(odd_ref, shared_ref, sums_ref, from_a_ref, from_b_ref, acc) + potential_ref[...] * waves
    first = (applied - window_ref[0] * waves) * (sigma_one / jnp.full((1, LANES), window_ref[1], f32))
    rows_ref[...] = first.astype(bf16).astype(f32)
    send_lists(rows_ref, odd_ref, shared_ref, a_ref, b_ref, stage)


def second_kernel(
    odd_ref, shared_ref, window_ref, sums_ref, from_a_ref, from_b_ref, waves_ref, first_ref, potential_ref,
    rows_ref, a_ref, b_ref, packed_ref, local_ref, filtered_ref, stage, *acc
):
    first = first_ref[...]
    potential = potential_ref[...]
    applied = assembled(odd_ref, shared_ref, sums_ref, from_a_ref, from_b_ref, acc) + potential * first
    gain = 2.0 * sigma_two / jnp.full((1, LANES), window_ref[1], f32)
    filtered = (applied - window_ref[0] * first) * gain - (sigma_one * sigma_two) * waves_ref[...]
    rounded = filtered.astype(bf16).astype(f32)
    rows_ref[...] = rounded
    send_lists(rows_ref, odd_ref, shared_ref, a_ref, b_ref, stage)
    term = potential * filtered
    half = a_ref.shape[0]
    for m in range(rounded.shape[0] // (2 * half)):
        rows = slice(2 * half * m, 2 * half * (m + 1))
        packed_ref[pl.ds(half * (m + 1), half), :] = pack(rounded[rows]).astype(bf16)
        local_ref[pl.ds(half * m, half), :] = pack(term[rows])
    filtered_ref[...] = jnp.transpose(filtered)[:HALF]


def block_of(left_side, part):
    both = jnp.dot(left_side, part, preferred_element_type=f32)
    both = both[:LANES] + both[LANES:]
    return jnp.transpose(both + swap(pltpu.roll(both, HALF, 0)))[:HALF]


def product_kernel(sums_ref, local_ref, own_ref, core_ref, far_ref, blocks_ref, left_ref):
    edge = (sums_ref.shape[0] - local_ref.shape[0]) // 2
    inner = sums_ref.shape[0] - edge
    sums = jnp.concatenate(
        [sums_ref[0:edge, :], sums_ref[edge:inner, :] + local_ref[...], sums_ref[inner:, :]], axis=0
    )
    turned = jnp.transpose(sums)
    coarse = turned.astype(bf16)
    fine = (turned - coarse.astype(f32)).astype(bf16)
    left_side = jnp.concatenate([coarse, fine], axis=0)
    left_ref[...] = left_side
    for n, ref in enumerate((own_ref, core_ref, far_ref)):
        blocks_ref[pl.ds(n * HALF, HALF), :] = block_of(left_side, ref[...])


def arrange_kernel(places_ref, left_ref, blocks_ref, part_ref, out_ref, product):
    count = product.shape[0] // HALF
    for n in range(count):
        at = pl.multiple_of(places_ref[n] * HALF, HALF)
        block = blocks_ref[pl.ds(n * HALF, HALF), :] if n < count - 1 else block_of(left_ref[...], part_ref[...])
        product[pl.ds(at, HALF), :] = block
    left = left_lanes()
    chunks = product.shape[0] // 4
    four = [product[pl.ds(r, chunks, stride=4), :] for r in range(4)]
    out_ref[:, 0:LANES] = jnp.where(left, four[0], swap(four[1]))
    out_ref[:, LANES : 2 * LANES] = jnp.where(left, four[2], swap(four[3]))


def local(waves, stiffness, cell_scale, potential, connect, live_cells, shared, window):
    columns, owned = waves.shape
    ghost = shared.shape[2]
    half = ghost // 2
    extended = owned + 2 * ghost
    nodes = connect.shape[0]
    cell_count = lax.axis_size("cells")
    band_count = lax.axis_size("bands")
    shared_list = shared.reshape(-1)
    index = jnp.pad(connect.T, ((0, 0), (0, LANES - nodes))).reshape(-1)
    stiff = jnp.pad(stiffness.astype(bf16), ((0, LANES - nodes), (0, LANES - nodes)))
    potential_rows = jnp.broadcast_to(potential[:, None], (owned, LANES))
    odd = (lax.axis_index("cells") % 2).reshape(1).astype(jnp.int32)
    places = jnp.arange(band_count, dtype=jnp.int32) ^ lax.axis_index("bands").astype(jnp.int32)
    pairs = [
        [(i + side, i + 1 - side) for i in range(first, cell_count - 1, 2) for side in range(2)]
        for first in range(2)
    ]

    def exchange(a_list, b_list):
        return lax.ppermute(a_list, "cells", pairs[0]), lax.ppermute(b_list, "cells", pairs[1])

    def to_band(part, flip):
        return lax.ppermute(part, "bands", [(b, b ^ flip) for b in range(band_count)])

    rows_of = shape_of(owned, LANES, f32)
    list_of = shape_of(half, LANES, bf16)
    stage_of = pltpu.VMEM((half, LANES), f32)
    cell_scratch = [
        pltpu.SMEM((GROUP * LANES,), jnp.int32),
        pltpu.SMEM((GROUP * LANES,), jnp.int32),
        pltpu.SemaphoreType.DMA((2,)),
        pltpu.VMEM((extended, LANES), f32),
        pltpu.VMEM((PAIRS, LANES, LANES), f32),
        pltpu.VMEM((PAIRS, LANES, LANES), f32),
    ] + [pltpu.VMEM((extended, LANES), f32)] * GROUP
    node_scratch = [stage_of] + [pltpu.VMEM((owned, LANES), f32)] * 4

    def call(kernel, outs, scratch, smem, vmem, name, placed=(), limit=10, flops=0):
        return pl.pallas_call(
            kernel,
            out_shape=outs,
            in_specs=[SMEM] * len(smem) + [PLACED] * len(placed) + [VMEM] * len(vmem),
            out_specs=jax.tree.map(lambda _: VMEM, outs),
            scratch_shapes=scratch,
            compiler_params=pltpu.CompilerParams(vmem_limit_bytes=limit << 20),
            cost_estimate=pl.CostEstimate(flops=flops, transcendentals=0, bytes_accessed=4 << 20),
            name=name,
        )(*smem, *placed, *vmem)

    waves_rows, *lists = call(
        prepare_kernel, (rows_of, list_of, list_of), [stage_of], (odd, shared_list), (waves,), "prepare"
    )
    tables = (odd, live_cells, cell_scale)
    work = dict(placed=(index,), limit=18, flops=20 * 10**9)
    edge_of = shape_of(half, LANES, f32)

    def cells(rows, lists):
        sums, *edges = call(
            cells_kernel, (rows_of, edge_of, edge_of), cell_scratch, tables, (stiff, rows, *lists), "cells", **work
        )
        return sums, *exchange(*edges)

    sums = cells(waves_rows, exchange(*lists))
    first_rows, *lists = call(
        first_kernel, (rows_of, list_of, list_of), node_scratch, (odd, shared_list, window),
        (*sums, waves_rows, potential_rows), "first",
    )
    sums = cells(first_rows, exchange(*lists))
    rounded_rows, a_list, b_list, packed, term, filtered = call(
        second_kernel,
        (
            rows_of, list_of, list_of, shape_of(extended // 2, LANES, bf16),
            shape_of(owned // 2, LANES, f32), shape_of(columns, owned, f32),
        ),
        node_scratch, (odd, shared_list, window),
        (*sums, waves_rows, first_rows, potential_rows), "second",
    )
    lists = exchange(a_list, b_list)
    packed = lax.dynamic_update_slice(packed, lists[0], (0, 0))
    packed = lax.dynamic_update_slice(packed, lists[1], (half + owned // 2, 0))
    far = to_band(packed, 2)
    core = to_band(packed, 1)
    packed_sums = call(
        last_cells_kernel, shape_of(extended // 2, LANES, f32), cell_scratch, tables,
        (stiff, rounded_rows, *lists), "last_cells", **work,
    )
    far, packed_sums = lax.optimization_barrier((far, packed_sums))
    other = to_band(far, 1)
    waves_all = columns * band_count
    blocks, left_side = call(
        product_kernel, (shape_of(waves_all - HALF, LANES, f32), shape_of(2 * LANES, extended // 2, bf16)),
        [], (), (packed_sums, term, packed, core, far), "product",
    )
    partial_value = call(
        arrange_kernel, shape_of(waves_all // 4, 4 * HALF, f32),
        [pltpu.VMEM((waves_all, LANES), f32)], (places,), (left_side, blocks, other), "arrange",
    )
    arrived = lax.all_to_all(partial_value, "cells", split_axis=0, concat_axis=0, tiled=True)
    own_rows = waves_all // cell_count
    projected = (arrived.sum(axis=0) * (1.0 / (owned * cell_count))).reshape(own_rows, columns)
    return (filtered, projected)


def solution(mesh):
    return jax.shard_map(
        local,
        mesh=mesh,
        in_specs=(
            P("bands", "cells"),
            P(),
            P("cells"),
            P("cells"),
            P(None, "cells"),
            P("cells"),
            P("cells", None, None),
            P(),
        ),
        out_specs=(P("bands", "cells"), P("cells", "bands")),
        check_vma=False,
    )
```

```python
import jax
import jax.numpy as jnp
from jax import lax
from jax.experimental import pallas as pl
from jax.experimental.pallas import tpu as pltpu
from jax.sharding import PartitionSpec as P

sigma_one = -0.5
sigma_two = 1.0 / (2.0 / sigma_one - sigma_one)


LANES = 128
HALF = 64
GROUP = 8
PAIRS = GROUP // 2
NODES = 125

VMEM = pl.BlockSpec(memory_space=pltpu.VMEM)
SMEM = pl.BlockSpec(memory_space=pltpu.SMEM)
PLACED = pl.BlockSpec(memory_space=pl.ANY)
f32 = jnp.float32
bf16 = jnp.bfloat16


def shape_of(rows, lanes, dtype):
    return jax.ShapeDtypeStruct((rows, lanes), dtype)


def left_lanes():
    return lax.broadcasted_iota(jnp.int32, (1, LANES), 1) < HALF


def swap(x):
    return pltpu.roll(x, HALF, 1)


def pack(rows):
    half = rows.shape[0] // 2
    return jnp.where(left_lanes(), rows[:half], rows[half:])


def unpack(x):
    left = left_lanes()
    other = swap(x)
    return jnp.where(left, x, other), jnp.where(left, other, x)


def pick_rows(values, list_ref, base, stage):
    left = left_lanes()
    count = stage.shape[0]
    for k in range(count):
        one = values[pl.ds(list_ref[base + k], 1), :]
        two = values[pl.ds(list_ref[base + count + k], 1), :]
        stage[pl.ds(k, 1), :] = jnp.where(left, one, two)


def send_lists(values, list_ref, a_ref, b_ref, stage):
    for side, ref in enumerate((a_ref, b_ref)):
        pick_rows(values, list_ref, 2 * stage.shape[0] * side, stage)
        ref[...] = stage[...].astype(bf16)


def prepare_kernel(list_ref, waves_ref, rows_ref, a_ref, b_ref, stage):
    block = waves_ref[...].astype(f32)
    rows_ref[...] = jnp.transpose(jnp.concatenate([block, block], axis=0))
    send_lists(rows_ref, list_ref, a_ref, b_ref, stage)


def cell_sums(odd_ref, live_ref, scale_ref, index_ref, stiff_ref, own_ref, a_ref, b_ref, slots, sems, x, blocks, acc):
    left = left_lanes()
    half = a_ref.shape[0]
    ghost = 2 * half
    owned = own_ref.shape[0]
    extended = x.shape[0]
    groups = scale_ref.shape[0] // GROUP
    size = slots[0].shape[0]
    g_even, p_even, g_odd, p_odd = blocks

    def fetch(group, n):
        first = pl.multiple_of(jnp.minimum(group, groups - 1) * size, size)
        return pltpu.make_async_copy(index_ref.at[pl.ds(first, size)], slots[n], sems.at[n])

    for n in range(4):
        fetch(n // 2, n).start()
    x[pl.ds(ghost, owned), :] = own_ref[...]
    edges = [pl.multiple_of(side * (ghost + owned), 8) for side in (1 - odd_ref[0], odd_ref[0])]
    for first, ref in zip(edges, (a_ref, b_ref)):
        one, two = unpack(ref[...].astype(f32))
        x[pl.ds(first, half), :] = one
        x[pl.ds(first + half, half), :] = two
    for g in (g_even, g_odd):
        for q in range(PAIRS):
            g[q, 120:128, :] = jnp.zeros((8, LANES), f32)
    live = live_ref[0]
    stiff = stiff_ref[...]

    def gather(i, slot, g):
        for q in range(PAIRS):
            one = x[pl.ds(slot[2 * q * LANES + i], 1), :]
            two = x[pl.ds(slot[(2 * q + 1) * LANES + i], 1), :]
            g[q, pl.ds(i, 1), :] = jnp.where(left, one, two)

    def scatter(i, slot, p):
        rows = [p[q, pl.ds(i, 1), :] for q in range(PAIRS)]
        for k in range(GROUP):
            acc[k][pl.ds(slot[k * LANES + i], 1), :] += rows[k // 2]

    def multiply(group, g, p):
        for q in range(0, PAIRS, 2):
            both = jnp.concatenate([g[q].astype(bf16), g[q + 1].astype(bf16)], axis=1)
            product = jnp.dot(stiff, both, preferred_element_type=f32)
            for h in range(2):
                cell = group * GROUP + 2 * (q + h)
                one = jnp.where(cell < live, scale_ref[cell], 0.0)
                two = jnp.where(cell + 1 < live, scale_ref[cell + 1], 0.0)
                p[q + h] = product[:, h * LANES : (h + 1) * LANES] * jnp.where(left, one, two)

    fetch(0, 0).wait()
    for i in range(NODES):
        gather(i, slots[0], g_even)
        for a in acc:
            if i * 32 < extended:
                rows = min(32, extended - i * 32)
                a[pl.ds(i * 32, rows), :] = jnp.zeros((rows, LANES), f32)
    fetch(2, 0).start()

    def even_half(turn):
        fetch(0, 1).wait()
        fetch(0, 2).wait()
        multiply(2 * turn, g_even, p_even)
        for i in range(NODES):
            scatter(i, slots[1], p_even)
            gather(i, slots[2], g_odd)
        fetch(2 * turn + 2, 1).start()
        fetch(2 * turn + 3, 2).start()
        fetch(0, 3).wait()

    def two_groups(turn, carry):
        even_half(turn)
        fetch(0, 0).wait()
        multiply(2 * turn + 1, g_odd, p_odd)
        for i in range(NODES):
            scatter(i, slots[3], p_odd)
            gather(i, slots[0], g_even)
        fetch(2 * turn + 3, 3).start()
        fetch(2 * turn + 4, 0).start()
        return carry

    last = (live + 2 * GROUP - 1) // (2 * GROUP) - 1
    lax.fori_loop(0, last, two_groups, 0)
    even_half(last)
    multiply(2 * last + 1, g_odd, p_odd)
    for i in range(NODES):
        scatter(i, slots[3], p_odd)
    for n in range(3):
        fetch(0, n).wait()

    def total(first, count):
        one = acc[0][pl.ds(first, count), :]
        two = acc[1][pl.ds(first, count), :]
        for q in range(1, PAIRS):
            one = one + acc[2 * q][pl.ds(first, count), :]
            two = two + acc[2 * q + 1][pl.ds(first, count), :]
        both = jnp.where(left, one, two)
        return both + swap(both)

    return total(ghost, owned), *(pack(total(first, ghost)) for first in edges)


def cell_scratch_of(extended):
    return (
        [pltpu.SMEM((GROUP * LANES,), jnp.int32)] * 4
        + [pltpu.SemaphoreType.DMA((4,)), pltpu.VMEM((extended, LANES), f32)]
        + [pltpu.VMEM((PAIRS, LANES, LANES), f32)] * 4
        + [pltpu.VMEM((extended, LANES), f32)] * GROUP
    )


def split(scratch):
    return scratch[:4], scratch[4], scratch[5], scratch[6:10], scratch[10:]


def cells_kernel(*refs):
    ins, (sums_ref, a_ref, b_ref), scratch = refs[:8], refs[8:11], refs[11:]
    sums_ref[...], a_ref[...], b_ref[...] = cell_sums(*ins, *split(scratch))


def last_cells_kernel(*refs):
    ins, packed_ref, scratch = refs[:8], refs[8], refs[9:]
    sums, a_part, b_part = cell_sums(*ins, *split(scratch))
    half = a_part.shape[0]
    own = sums.shape[0] // 2
    packed_ref[pl.ds(0, half), :] = a_part
    for m in range(own // half):
        packed_ref[pl.ds(half + m * half, half), :] = pack(sums[2 * half * m : 2 * half * (m + 1)])
    packed_ref[pl.ds(half + own, half), :] = b_part


def assembled(list_ref, sums_ref, a_ref, b_ref, acc):
    left = left_lanes()
    count = a_ref.shape[0]
    for a in acc:
        a[...] = jnp.zeros_like(a)
    for k in range(count):
        for side, ref in enumerate((a_ref, b_ref)):
            row = ref[pl.ds(k, 1), :]
            for part in range(2):
                at = list_ref[2 * count * side + count * part + k]
                acc[2 * side + part][pl.ds(at, 1), :] += row
    both = jnp.where(left, acc[0][...] + acc[2][...], acc[1][...] + acc[3][...])
    return sums_ref[...] + (both + swap(both))


def first_kernel(
    list_ref, window_ref, sums_ref, from_a_ref, from_b_ref, waves_ref, potential_ref,
    rows_ref, a_ref, b_ref, stage, *acc
):
    waves = waves_ref[...]
    applied = assembled(list_ref, sums_ref, from_a_ref, from_b_ref, acc) + potential_ref[...] * waves
    first = (applied - window_ref[0] * waves) * (sigma_one / jnp.full((1, LANES), window_ref[1], f32))
    rows_ref[...] = first.astype(bf16).astype(f32)
    send_lists(rows_ref, list_ref, a_ref, b_ref, stage)


def second_kernel(
    list_ref, window_ref, sums_ref, from_a_ref, from_b_ref, waves_ref, first_ref, potential_ref,
    rows_ref, a_ref, b_ref, packed_ref, local_ref, filtered_ref, stage, *acc
):
    first = first_ref[...]
    potential = potential_ref[...]
    applied = assembled(list_ref, sums_ref, from_a_ref, from_b_ref, acc) + potential * first
    gain = 2.0 * sigma_two / jnp.full((1, LANES), window_ref[1], f32)
    filtered = (applied - window_ref[0] * first) * gain - (sigma_one * sigma_two) * waves_ref[...]
    rounded = filtered.astype(bf16).astype(f32)
    rows_ref[...] = rounded
    send_lists(rows_ref, list_ref, a_ref, b_ref, stage)
    term = potential * filtered
    half = a_ref.shape[0]
    for m in range(rounded.shape[0] // (2 * half)):
        rows = slice(2 * half * m, 2 * half * (m + 1))
        packed_ref[pl.ds(half * (m + 1), half), :] = pack(rounded[rows]).astype(bf16)
        local_ref[pl.ds(half * m, half), :] = pack(term[rows])
    filtered_ref[...] = jnp.transpose(filtered)[:HALF]


def block_of(left_side, part):
    both = jnp.dot(left_side, part, preferred_element_type=f32)
    both = both[:LANES] + both[LANES:]
    return jnp.transpose(both + swap(pltpu.roll(both, HALF, 0)))[:HALF]


def product_kernel(sums_ref, local_ref, own_ref, core_ref, far_ref, blocks_ref, left_ref):
    edge = (sums_ref.shape[0] - local_ref.shape[0]) // 2
    inner = sums_ref.shape[0] - edge
    sums = jnp.concatenate(
        [sums_ref[0:edge, :], sums_ref[edge:inner, :] + local_ref[...], sums_ref[inner:, :]], axis=0
    )
    turned = jnp.transpose(sums)
    coarse = turned.astype(bf16)
    fine = (turned - coarse.astype(f32)).astype(bf16)
    left_side = jnp.concatenate([coarse, fine], axis=0)
    left_ref[...] = left_side
    for n, ref in enumerate((own_ref, core_ref, far_ref)):
        blocks_ref[pl.ds(n * HALF, HALF), :] = block_of(left_side, ref[...])


def arrange_kernel(places_ref, left_ref, blocks_ref, part_ref, out_ref, product):
    count = product.shape[0] // HALF
    for n in range(count):
        at = pl.multiple_of(places_ref[n] * HALF, HALF)
        block = blocks_ref[pl.ds(n * HALF, HALF), :] if n < count - 1 else block_of(left_ref[...], part_ref[...])
        product[pl.ds(at, HALF), :] = block
    left = left_lanes()
    chunks = product.shape[0] // 4
    four = [product[pl.ds(r, chunks, stride=4), :] for r in range(4)]
    out_ref[:, 0:LANES] = jnp.where(left, four[0], swap(four[1]))
    out_ref[:, LANES : 2 * LANES] = jnp.where(left, four[2], swap(four[3]))


def local(waves, stiffness, cell_scale, potential, connect, live_cells, shared, window):
    columns, owned = waves.shape
    ghost = shared.shape[2]
    half = ghost // 2
    extended = owned + 2 * ghost
    nodes = connect.shape[0]
    cell_count = lax.axis_size("cells")
    band_count = lax.axis_size("bands")
    index = jnp.pad(connect.T, ((0, 0), (0, LANES - nodes))).reshape(-1)
    stiff = jnp.pad(stiffness.astype(bf16), ((0, LANES - nodes), (0, LANES - nodes)))
    potential_rows = jnp.broadcast_to(potential[:, None], (owned, LANES))
    odd = (lax.axis_index("cells") % 2).reshape(1).astype(jnp.int32)
    shared_list = jnp.where(odd[:, None] == 1, shared[0], shared[0, ::-1]).reshape(-1)
    places = jnp.arange(band_count, dtype=jnp.int32) ^ lax.axis_index("bands").astype(jnp.int32)
    pairs = [
        [(i + side, i + 1 - side) for i in range(first, cell_count - 1, 2) for side in range(2)]
        for first in range(2)
    ]

    def exchange(a_list, b_list):
        return lax.ppermute(a_list, "cells", pairs[0]), lax.ppermute(b_list, "cells", pairs[1])

    def to_band(part, flip):
        return lax.ppermute(part, "bands", [(b, b ^ flip) for b in range(band_count)])

    rows_of = shape_of(owned, LANES, f32)
    list_of = shape_of(half, LANES, bf16)
    stage_of = pltpu.VMEM((half, LANES), f32)
    cell_scratch = cell_scratch_of(extended)
    node_scratch = [stage_of] + [pltpu.VMEM((owned, LANES), f32)] * 4

    def call(kernel, outs, scratch, smem, vmem, name, placed=(), limit=10, flops=0):
        return pl.pallas_call(
            kernel,
            out_shape=outs,
            in_specs=[SMEM] * len(smem) + [PLACED] * len(placed) + [VMEM] * len(vmem),
            out_specs=jax.tree.map(lambda _: VMEM, outs),
            scratch_shapes=scratch,
            compiler_params=pltpu.CompilerParams(vmem_limit_bytes=limit << 20),
            cost_estimate=pl.CostEstimate(flops=flops, transcendentals=0, bytes_accessed=4 << 20),
            name=name,
        )(*smem, *placed, *vmem)

    waves_rows, *lists = call(
        prepare_kernel, (rows_of, list_of, list_of), [stage_of], (shared_list,), (waves,), "prepare"
    )
    tables = (odd, live_cells, cell_scale)
    work = dict(placed=(index,), limit=18, flops=20 * 10**9)
    edge_of = shape_of(half, LANES, f32)

    def cells(rows, lists):
        sums, *edges = call(
            cells_kernel, (rows_of, edge_of, edge_of), cell_scratch, tables, (stiff, rows, *lists), "cells", **work
        )
        return sums, *exchange(*edges)

    sums = cells(waves_rows, exchange(*lists))
    first_rows, *lists = call(
        first_kernel, (rows_of, list_of, list_of), node_scratch, (shared_list, window),
        (*sums, waves_rows, potential_rows), "first",
    )
    sums = cells(first_rows, exchange(*lists))
    rounded_rows, a_list, b_list, packed, term, filtered = call(
        second_kernel,
        (
            rows_of, list_of, list_of, shape_of(extended // 2, LANES, bf16),
            shape_of(owned // 2, LANES, f32), shape_of(columns, owned, f32),
        ),
        node_scratch, (shared_list, window),
        (*sums, waves_rows, first_rows, potential_rows), "second",
    )
    lists = exchange(a_list, b_list)
    packed = lax.dynamic_update_slice(packed, lists[0], (0, 0))
    packed = lax.dynamic_update_slice(packed, lists[1], (half + owned // 2, 0))
    far = to_band(packed, 2)
    core = to_band(packed, 1)
    packed_sums = call(
        last_cells_kernel, shape_of(extended // 2, LANES, f32), cell_scratch, tables,
        (stiff, rounded_rows, *lists), "last_cells", **work,
    )
    far, packed_sums = lax.optimization_barrier((far, packed_sums))
    other = to_band(far, 1)
    waves_all = columns * band_count
    blocks, left_side = call(
        product_kernel, (shape_of(waves_all - HALF, LANES, f32), shape_of(2 * LANES, extended // 2, bf16)),
        [], (), (packed_sums, term, packed, core, far), "product",
    )
    partial_value = call(
        arrange_kernel, shape_of(waves_all // 4, 4 * HALF, f32),
        [pltpu.VMEM((waves_all, LANES), f32)], (places,), (left_side, blocks, other), "arrange",
    )
    arrived = lax.all_to_all(partial_value, "cells", split_axis=0, concat_axis=0, tiled=True)
    own_rows = waves_all // cell_count
    projected = (arrived.sum(axis=0) * (1.0 / (owned * cell_count))).reshape(own_rows, columns)
    return (filtered, projected)


def solution(mesh):
    return jax.shard_map(
        local,
        mesh=mesh,
        in_specs=(
            P("bands", "cells"),
            P(),
            P("cells"),
            P("cells"),
            P(None, "cells"),
            P("cells"),
            P("cells", None, None),
            P(),
        ),
        out_specs=(P("bands", "cells"), P("cells", "bands")),
        check_vma=False,
    )
```

```python
import jax
import jax.numpy as jnp
from jax import lax
from jax.experimental import pallas as pl
from jax.experimental.pallas import tpu as pltpu
from jax.sharding import PartitionSpec as P

sigma_one = -0.5
sigma_two = 1.0 / (2.0 / sigma_one - sigma_one)


LANES = 128
HALF = 64
GROUP = 8
PAIRS = GROUP // 2
NODES = 125
WINDOW = 128

VMEM = pl.BlockSpec(memory_space=pltpu.VMEM)
SMEM = pl.BlockSpec(memory_space=pltpu.SMEM)
PLACED = pl.BlockSpec(memory_space=pl.ANY)
f32 = jnp.float32
bf16 = jnp.bfloat16


def shape_of(rows, lanes, dtype):
    return jax.ShapeDtypeStruct((rows, lanes), dtype)


def left_lanes():
    return lax.broadcasted_iota(jnp.int32, (1, LANES), 1) < HALF


def swap(x):
    return pltpu.roll(x, HALF, 1)


def pack(rows):
    half = rows.shape[0] // 2
    return jnp.where(left_lanes(), rows[:half], rows[half:])


def unpack(x):
    left = left_lanes()
    other = swap(x)
    return jnp.where(left, x, other), jnp.where(left, other, x)


def pick_rows(values, list_ref, base, stage):
    left = left_lanes()
    count = stage.shape[0]
    for k in range(count):
        one = values[pl.ds(list_ref[base + k], 1), :]
        two = values[pl.ds(list_ref[base + count + k], 1), :]
        stage[pl.ds(k, 1), :] = jnp.where(left, one, two)


def send_lists(values, list_ref, a_ref, b_ref, stage):
    for side, ref in enumerate((a_ref, b_ref)):
        pick_rows(values, list_ref, 2 * stage.shape[0] * side, stage)
        ref[...] = stage[...].astype(bf16)


def prepare_kernel(list_ref, waves_ref, rows_ref, a_ref, b_ref, stage):
    block = waves_ref[...].astype(f32)
    rows_ref[...] = jnp.transpose(jnp.concatenate([block, block], axis=0))
    send_lists(rows_ref, list_ref, a_ref, b_ref, stage)


def cell_sums(below_ref, live_ref, table_ref, index_ref, stiff_ref, own_ref, a_ref, b_ref, slots, sems, x, blocks, acc):
    left = left_lanes()
    half = a_ref.shape[0]
    ghost = 2 * half
    owned = own_ref.shape[0]
    extended = x.shape[0]
    size = slots[0].shape[0]
    groups = index_ref.shape[0] // size
    g_even, p_even, g_odd, p_odd = blocks

    def fetch(group, n):
        first = pl.multiple_of(jnp.minimum(group, groups - 1) * size, size)
        return pltpu.make_async_copy(index_ref.at[pl.ds(first, size)], slots[n], sems.at[n])

    for n in range(4):
        fetch(n // 2, n).start()
    x[pl.ds(ghost, owned), :] = own_ref[...]
    edges = [pl.multiple_of(side * (ghost + owned), 8) for side in (1 - below_ref[0], below_ref[0])]
    for first, ref in zip(edges, (a_ref, b_ref)):
        one, two = unpack(ref[...].astype(f32))
        x[pl.ds(first, half), :] = one
        x[pl.ds(first + half, half), :] = two
    for g in (g_even, g_odd):
        for q in range(PAIRS):
            g[q, 120:128, :] = jnp.zeros((8, LANES), f32)
    live = live_ref[0]
    stiff = stiff_ref[...]

    def gather(i, slot, g):
        for q in range(PAIRS):
            one = x[pl.ds(slot[2 * q * LANES + i], 1), :]
            two = x[pl.ds(slot[(2 * q + 1) * LANES + i], 1), :]
            g[q, pl.ds(i, 1), :] = jnp.where(left, one, two)

    def scatter(i, slot, p):
        rows = [p[q, pl.ds(i, 1), :] for q in range(PAIRS)]
        for k in range(GROUP):
            acc[k][pl.ds(slot[k * LANES + i], 1), :] += rows[k // 2]

    def multiply(group, g, p):
        for q in range(0, PAIRS, 2):
            both = jnp.concatenate([g[q].astype(bf16), g[q + 1].astype(bf16)], axis=1)
            product = jnp.dot(stiff, both, preferred_element_type=f32)
            for h in range(2):
                cell = group * GROUP + 2 * (q + h)
                weight = jnp.where(left, table_ref[cell], table_ref[cell + 1])
                p[q + h] = product[:, h * LANES : (h + 1) * LANES] * weight

    fetch(0, 0).wait()
    for i in range(NODES):
        gather(i, slots[0], g_even)
        for a in acc:
            if i * 32 < extended:
                rows = min(32, extended - i * 32)
                a[pl.ds(i * 32, rows), :] = jnp.zeros((rows, LANES), f32)
    fetch(2, 0).start()

    def even_half(turn):
        fetch(0, 1).wait()
        fetch(0, 2).wait()
        multiply(2 * turn, g_even, p_even)
        for i in range(NODES):
            scatter(i, slots[1], p_even)
            gather(i, slots[2], g_odd)
        fetch(2 * turn + 2, 1).start()
        fetch(2 * turn + 3, 2).start()
        fetch(0, 3).wait()

    def two_groups(turn, carry):
        even_half(turn)
        fetch(0, 0).wait()
        multiply(2 * turn + 1, g_odd, p_odd)
        for i in range(NODES):
            scatter(i, slots[3], p_odd)
            gather(i, slots[0], g_even)
        fetch(2 * turn + 3, 3).start()
        fetch(2 * turn + 4, 0).start()
        return carry

    last = (live + 2 * GROUP - 1) // (2 * GROUP) - 1
    lax.fori_loop(0, last, two_groups, 0)
    even_half(last)
    multiply(2 * last + 1, g_odd, p_odd)
    for i in range(NODES):
        scatter(i, slots[3], p_odd)
    for n in range(3):
        fetch(0, n).wait()

    def total(first, count):
        one = acc[0][pl.ds(first, count), :]
        two = acc[1][pl.ds(first, count), :]
        for q in range(1, PAIRS):
            one = one + acc[2 * q][pl.ds(first, count), :]
            two = two + acc[2 * q + 1][pl.ds(first, count), :]
        both = jnp.where(left, one, two)
        return both + swap(both)

    return total(ghost, owned), *(pack(total(first, ghost)) for first in edges)


def cell_scratch_of(extended):
    return (
        [pltpu.SMEM((GROUP * LANES,), jnp.int32)] * 4
        + [pltpu.SemaphoreType.DMA((4,)), pltpu.VMEM((extended, LANES), f32)]
        + [pltpu.VMEM((PAIRS, LANES, LANES), f32)] * 4
        + [pltpu.VMEM((extended, LANES), f32)] * GROUP
    )


def split(scratch):
    return scratch[:4], scratch[4], scratch[5], scratch[6:10], scratch[10:]


def cells_kernel(*refs):
    ins, (sums_ref, a_ref, b_ref), scratch = refs[:8], refs[8:11], refs[11:]
    sums_ref[...], a_ref[...], b_ref[...] = cell_sums(*ins, *split(scratch))


def last_cells_kernel(*refs):
    ins, packed_ref, scratch = refs[:8], refs[8], refs[9:]
    sums, a_part, b_part = cell_sums(*ins, *split(scratch))
    half = a_part.shape[0]
    own = sums.shape[0] // 2
    packed_ref[pl.ds(0, half), :] = a_part
    for m in range(own // half):
        packed_ref[pl.ds(half + m * half, half), :] = pack(sums[2 * half * m : 2 * half * (m + 1)])
    packed_ref[pl.ds(half + own, half), :] = b_part


def assembled(list_ref, sums_ref, a_ref, b_ref, acc):
    left = left_lanes()
    count = a_ref.shape[0]
    for a in acc:
        a[...] = jnp.zeros_like(a)
    for k in range(count):
        for side, ref in enumerate((a_ref, b_ref)):
            row = ref[pl.ds(k, 1), :]
            for part in range(2):
                at = list_ref[2 * count * side + count * part + k]
                acc[2 * side + part][pl.ds(at, 1), :] += row
    both = jnp.where(left, acc[0][...] + acc[2][...], acc[1][...] + acc[3][...])
    return sums_ref[...] + (both + swap(both))


def first_kernel(
    list_ref, table_ref, sums_ref, from_a_ref, from_b_ref, waves_ref, potential_ref,
    rows_ref, a_ref, b_ref, stage, *acc
):
    waves = waves_ref[...]
    applied = assembled(list_ref, sums_ref, from_a_ref, from_b_ref, acc) + potential_ref[...] * waves
    first = (applied - table_ref[WINDOW] * waves) * (sigma_one / jnp.full((1, LANES), table_ref[WINDOW + 1], f32))
    rows_ref[...] = first.astype(bf16).astype(f32)
    send_lists(rows_ref, list_ref, a_ref, b_ref, stage)


def second_kernel(
    list_ref, table_ref, sums_ref, from_a_ref, from_b_ref, waves_ref, first_ref, potential_ref,
    rows_ref, a_ref, b_ref, packed_ref, local_ref, filtered_ref, stage, *acc
):
    first = first_ref[...]
    potential = potential_ref[...]
    applied = assembled(list_ref, sums_ref, from_a_ref, from_b_ref, acc) + potential * first
    gain = 2.0 * sigma_two / jnp.full((1, LANES), table_ref[WINDOW + 1], f32)
    filtered = (applied - table_ref[WINDOW] * first) * gain - (sigma_one * sigma_two) * waves_ref[...]
    rounded = filtered.astype(bf16).astype(f32)
    rows_ref[...] = rounded
    send_lists(rows_ref, list_ref, a_ref, b_ref, stage)
    term = potential * filtered
    half = a_ref.shape[0]
    for m in range(rounded.shape[0] // (2 * half)):
        rows = slice(2 * half * m, 2 * half * (m + 1))
        packed_ref[pl.ds(half * (m + 1), half), :] = pack(rounded[rows]).astype(bf16)
        local_ref[pl.ds(half * m, half), :] = pack(term[rows])
    filtered_ref[...] = jnp.transpose(filtered)[:HALF]


def block_of(left_side, part):
    both = jnp.dot(left_side, part, preferred_element_type=f32)
    both = both[:LANES] + both[LANES:]
    return jnp.transpose(both + swap(pltpu.roll(both, HALF, 0)))[:HALF]


def product_kernel(sums_ref, local_ref, own_ref, core_ref, far_ref, blocks_ref, left_ref):
    edge = (sums_ref.shape[0] - local_ref.shape[0]) // 2
    inner = sums_ref.shape[0] - edge
    sums = jnp.concatenate(
        [sums_ref[0:edge, :], sums_ref[edge:inner, :] + local_ref[...], sums_ref[inner:, :]], axis=0
    )
    turned = jnp.transpose(sums)
    coarse = turned.astype(bf16)
    fine = (turned - coarse.astype(f32)).astype(bf16)
    left_side = jnp.concatenate([coarse, fine], axis=0)
    left_ref[...] = left_side
    for n, ref in enumerate((own_ref, core_ref, far_ref)):
        blocks_ref[pl.ds(n * HALF, HALF), :] = block_of(left_side, ref[...])


def arrange_kernel(places_ref, left_ref, blocks_ref, part_ref, out_ref, product):
    count = product.shape[0] // HALF
    for n in range(count):
        at = pl.multiple_of(places_ref[n] * HALF, HALF)
        block = blocks_ref[pl.ds(n * HALF, HALF), :] if n < count - 1 else block_of(left_ref[...], part_ref[...])
        product[pl.ds(at, HALF), :] = block
    left = left_lanes()
    chunks = product.shape[0] // 4
    four = [product[pl.ds(r, chunks, stride=4), :] for r in range(4)]
    out_ref[:, 0:LANES] = jnp.where(left, four[0], swap(four[1]))
    out_ref[:, LANES : 2 * LANES] = jnp.where(left, four[2], swap(four[3]))


def local(waves, stiffness, cell_scale, potential, connect, live_cells, shared, window):
    columns, owned = waves.shape
    ghost = shared.shape[2]
    half = ghost // 2
    extended = owned + 2 * ghost
    nodes = connect.shape[0]
    cell_count = lax.axis_size("cells")
    band_count = lax.axis_size("bands")
    index = jnp.pad(connect.T, ((0, 0), (0, LANES - nodes))).reshape(-1)
    stiff = jnp.pad(stiffness.astype(bf16), ((0, LANES - nodes), (0, LANES - nodes)))
    potential_rows = jnp.broadcast_to(potential[:, None], (owned, LANES))
    below = ((lax.axis_index("cells") + 1) % 2).reshape(1).astype(jnp.int32)
    shared_list = jnp.where(below[:, None] == 1, shared[0], shared[0, ::-1]).reshape(-1)
    alive = jnp.arange(cell_scale.shape[0]) < live_cells[0]
    table = jnp.concatenate([jnp.where(alive, cell_scale, 0.0), window])
    places = jnp.arange(band_count, dtype=jnp.int32) ^ lax.axis_index("bands").astype(jnp.int32)
    pairs = [
        [(i + side, i + 1 - side) for i in range(first, cell_count - 1, 2) for side in range(2)]
        for first in (1, 0)
    ]

    def exchange(a_list, b_list):
        return lax.ppermute(a_list, "cells", pairs[0]), lax.ppermute(b_list, "cells", pairs[1])

    def to_band(part, flip):
        return lax.ppermute(part, "bands", [(b, b ^ flip) for b in range(band_count)])

    rows_of = shape_of(owned, LANES, f32)
    list_of = shape_of(half, LANES, bf16)
    stage_of = pltpu.VMEM((half, LANES), f32)
    cell_scratch = cell_scratch_of(extended)
    node_scratch = [stage_of] + [pltpu.VMEM((owned, LANES), f32)] * 4

    def call(kernel, outs, scratch, smem, vmem, name, placed=(), limit=10, flops=0):
        return pl.pallas_call(
            kernel,
            out_shape=outs,
            in_specs=[SMEM] * len(smem) + [PLACED] * len(placed) + [VMEM] * len(vmem),
            out_specs=jax.tree.map(lambda _: VMEM, outs),
            scratch_shapes=scratch,
            compiler_params=pltpu.CompilerParams(vmem_limit_bytes=limit << 20),
            cost_estimate=pl.CostEstimate(flops=flops, transcendentals=0, bytes_accessed=4 << 20),
            name=name,
        )(*smem, *placed, *vmem)

    waves_rows, *lists = call(
        prepare_kernel, (rows_of, list_of, list_of), [stage_of], (shared_list,), (waves,), "prepare"
    )
    tables = (below, live_cells, table)
    work = dict(placed=(index,), limit=18, flops=20 * 10**9)
    edge_of = shape_of(half, LANES, f32)

    def cells(rows, lists):
        sums, *edges = call(
            cells_kernel, (rows_of, edge_of, edge_of), cell_scratch, tables, (stiff, rows, *lists), "cells", **work
        )
        return sums, *exchange(*edges)

    sums = cells(waves_rows, exchange(*lists))
    first_rows, *lists = call(
        first_kernel, (rows_of, list_of, list_of), node_scratch, (shared_list, table),
        (*sums, waves_rows, potential_rows), "first",
    )
    sums = cells(first_rows, exchange(*lists))
    rounded_rows, a_list, b_list, packed, term, filtered = call(
        second_kernel,
        (
            rows_of, list_of, list_of, shape_of(extended // 2, LANES, bf16),
            shape_of(owned // 2, LANES, f32), shape_of(columns, owned, f32),
        ),
        node_scratch, (shared_list, table),
        (*sums, waves_rows, first_rows, potential_rows), "second",
    )
    lists = exchange(a_list, b_list)
    packed = lax.dynamic_update_slice(packed, lists[0], (0, 0))
    packed = lax.dynamic_update_slice(packed, lists[1], (half + owned // 2, 0))
    far = to_band(packed, 2)
    core = to_band(packed, 1)
    packed_sums = call(
        last_cells_kernel, shape_of(extended // 2, LANES, f32), cell_scratch, tables,
        (stiff, rounded_rows, *lists), "last_cells", **work,
    )
    far, packed_sums = lax.optimization_barrier((far, packed_sums))
    other = to_band(far, 1)
    waves_all = columns * band_count
    blocks, left_side = call(
        product_kernel, (shape_of(waves_all - HALF, LANES, f32), shape_of(2 * LANES, extended // 2, bf16)),
        [], (), (packed_sums, term, packed, core, far), "product",
    )
    partial_value = call(
        arrange_kernel, shape_of(waves_all // 4, 4 * HALF, f32),
        [pltpu.VMEM((waves_all, LANES), f32)], (places,), (left_side, blocks, other), "arrange",
    )
    arrived = lax.all_to_all(partial_value, "cells", split_axis=0, concat_axis=0, tiled=True)
    own_rows = waves_all // cell_count
    projected = (arrived.sum(axis=0) * (1.0 / (owned * cell_count))).reshape(own_rows, columns)
    return (filtered, projected)


def solution(mesh):
    return jax.shard_map(
        local,
        mesh=mesh,
        in_specs=(
            P("bands", "cells"),
            P(),
            P("cells"),
            P("cells"),
            P(None, "cells"),
            P("cells"),
            P("cells", None, None),
            P(),
        ),
        out_specs=(P("bands", "cells"), P("cells", "bands")),
        check_vma=False,
    )
```
